32 devices in a mesh: frames: 4 (over x, core), codes: 8 (over z, y).
Axes of the slice: x: 2, y: 2, z: 4, core: 2. Of those that a mesh axis runs over, the one named last changes fastest.
Arguments:
- hidden: bfloat16 [16384, 1024], P('frames'), may hold values from -5 to 5
- head: bfloat16 [1024, 8192], P('frames', 'codes'), may hold values from -2 to 2
- chosen: int32 [8, 16384], P(None, 'frames'), may hold values from 0 to 1023
Outputs:
- confidence: float32 [8, 16384], P(None, 'frames')
- entropy: float32 [8, 16384], P(None, 'frames')
The draws below stay inside these ranges and needn't reach their ends.
All inputs are finite; a program needn't handle non-finite values.
Results may differ from the reference program's by a relative error of at most 0.0003.
Values may be sent and summed in bfloat16 or wider, within the bound.
No kernel may reach another device: no remote copies, remote signals or barrier semaphores. Data moves between devices by JAX's collectives and lax.ppermute only.
A program may use at most 64 MiB of HBM per device.

```python
import math
import jax
import jax.numpy as jnp

D = 1024
CODES = 1024
LEVELS = 8
FRAMES = 16384


def draw_hidden(key, part):
    seeded = jax.random.fold_in(key, 11)
    subkeys = jax.random.split(seeded, 2)
    values = jnp.clip(jax.random.normal(subkeys[1], (FRAMES, D), jnp.float32), -5.0, 5.0)
    return values.astype(jnp.bfloat16)


def draw_head(key, part):
    seeded = jax.random.fold_in(key, 13)
    subkeys = jax.random.split(seeded, 2)
    spread = 3.0 / math.sqrt(D)
    values = jnp.clip(jax.random.normal(subkeys[1], (D, LEVELS * CODES), jnp.float32) * spread, -6.0 * spread, 6.0 * spread)
    return values.astype(jnp.bfloat16)


def set_ends(values, own_key, low, largest):
    dims = values.shape
    index_at = [jax.random.randint(jax.random.fold_in(own_key, axis), (), 0, dims[axis]) for axis in range(len(dims))]
    values = values.at[tuple(index_at)].set(low)
    longest = dims.index(max(dims))
    index_at[longest] = (index_at[longest] + 1) % dims[longest]
    return values.at[tuple(index_at)].set(largest)


def setup_inputs(seed: int = 0) -> dict:
    arg_keys = jax.random.split(jax.random.key(seed), 4)
    return {
        "hidden": draw_hidden(jax.random.fold_in(arg_keys[3], 71), 0),
        "head": draw_head(jax.random.fold_in(arg_keys[3], 71), 0),
        "chosen": set_ends(jax.random.randint(arg_keys[2], (LEVELS, FRAMES), 0, CODES), jax.random.fold_in(arg_keys[2], 1), 0, CODES - 1).astype(jnp.int32),
    }


def reference(hidden, head, chosen):
    confidences = []
    entropies = []
    for level_id in range(LEVELS):
        head_slice = head[:, level_id * CODES:(level_id + 1) * CODES]
        scores = jnp.dot(hidden, head_slice, preferred_element_type=jnp.float32)
        highest = jnp.max(scores, axis=1)
        shifted = jnp.exp(scores - highest[:, None])
        exp_total = jnp.sum(shifted, axis=1)
        exp_logit = jnp.sum(shifted * scores, axis=1)
        log_total = highest + jnp.log(exp_total)
        wanted = chosen[level_id][:, None].astype(jnp.int32)
        picked = jnp.take_along_axis(scores, wanted, axis=1)[:, 0]
        confidences.append(picked - log_total)
        entropies.append(log_total - exp_logit / exp_total)
    return jnp.stack(confidences), jnp.stack(entropies)
```

```python
import functools

import jax
import jax.numpy as jnp
from jax import lax
from jax.experimental import pallas as pl
from jax.experimental.pallas import tpu as pltpu
from jax.sharding import PartitionSpec as P

CODES = 1024
TILE = 256
UNROLL = 4
SPLITS = (512, 512)
VMEM = pl.BlockSpec(memory_space=pltpu.VMEM)
SMEM = pl.BlockSpec(memory_space=pltpu.SMEM)


def flip(block, axis, bit):
    count = lax.axis_size(axis)
    return lax.ppermute(block, axis, [(i, i ^ 1 << bit) for i in range(count)])


def spread(pieces, axis, bits):
    for bit in bits:
        for offset in sorted(pieces):
            pieces[offset | 1 << bit] = flip(pieces[offset], axis, bit)
    return pieces


def in_vmem(shape, dtype):
    return pltpu.MemorySpace.VMEM(shape, dtype)


def partial_kernel(widths, place, hidden, own, sibling, *rest):
    outs, head_t = rest[:-1], rest[-1]
    rows = own.shape[0]
    core = place[0]
    head_t[:, pl.ds(pl.multiple_of(core * rows, rows), rows)] = own[...].T
    head_t[:, pl.ds(pl.multiple_of((1 - core) * rows, rows), rows)] = sibling[...].T
    span = 2 * rows
    depth = pl.ds(pl.multiple_of(place[1] * span, span), span)

    def body(step, carry):
        for lane in range(UNROLL):
            tile = pl.ds(pl.multiple_of((step * UNROLL + lane) * TILE, TILE), TILE)
            block = hidden[tile, depth]
            low = 0
            for out, width in zip(outs, widths):
                out[:, tile] = lax.dot_general(
                    head_t[low : low + width, :],
                    block,
                    (((1,), (1,)), ((), ())),
                    preferred_element_type=jnp.float32,
                )
                low += width
        return carry

    lax.fori_loop(0, hidden.shape[0] // (TILE * UNROLL), body, 0)


def partial_logits(place, hidden, own, sibling, widths):
    frames = hidden.shape[0]
    rows, columns = own.shape
    return pl.pallas_call(
        functools.partial(partial_kernel, widths),
        in_specs=[SMEM, VMEM, VMEM, VMEM],
        out_specs=[VMEM] * len(widths),
        out_shape=[pltpu.VMEM((width, frames), jnp.float32) for width in widths],
        scratch_shapes=[pltpu.VMEM((columns, 2 * rows), jnp.bfloat16)],
        compiler_params=pltpu.CompilerParams(vmem_limit_bytes=8 << 20),
        cost_estimate=pl.CostEstimate(
            flops=4 * frames * rows * columns, bytes_accessed=1 << 20, transcendentals=0
        ),
        name="partial",
    )(place, hidden, own, sibling)


def stats_kernel(pairs, first, last, base, place, hidden, part, chosen, *rest):
    pieces, rest = rest[: 2 * pairs], rest[2 * pairs :]
    before, rest = (None, rest) if first else (rest[0], rest[1:])
    out, head_t = rest
    rows, width = pieces[0].shape
    span = 2 * rows
    core = place[0]
    for pair in range(pairs):
        for side in range(2):
            spot = pl.multiple_of((core if side == 0 else 1 - core) * rows, rows)
            head_t[pair, :, pl.ds(spot, rows)] = pieces[2 * pair + side][...].T
    sublane = lax.broadcasted_iota(jnp.int32, (8, TILE), 0) + base

    def body(step, carry):
        for lane in range(UNROLL):
            tile = pl.ds(pl.multiple_of((step * UNROLL + lane) * TILE, TILE), TILE)
            logits = part[:, tile]
            for pair in range(pairs):
                depth = pl.ds(pl.multiple_of((place[1] ^ (pair + 1)) * span, span), span)
                logits = logits + lax.dot_general(
                    head_t[pair],
                    hidden[tile, depth],
                    (((1,), (1,)), ((), ())),
                    preferred_element_type=jnp.float32,
                )
            highest = jnp.max(logits, axis=0, keepdims=True)
            if not first:
                highest = jnp.maximum(highest, before[0:1, tile])
            wanted = chosen[pl.ds(place[2], 1), tile] - place[3] - sublane
            total = jnp.zeros((8, TILE), jnp.float32)
            weighted, picked = total, total
            for row in range(0, width, 8):
                piece = logits[row : row + 8]
                below = piece - highest
                power = jnp.exp(below)
                total += power
                weighted += power * below
                picked = jnp.where(wanted == row, piece, picked)
            total = jnp.sum(total, axis=0, keepdims=True)
            weighted = jnp.sum(weighted, axis=0, keepdims=True)
            picked = jnp.sum(picked, axis=0, keepdims=True)
            if not first:
                drop = before[0:1, tile] - highest
                factor = jnp.exp(drop)
                total += factor * before[1:2, tile]
                weighted += factor * (before[2:3, tile] + drop * before[1:2, tile])
                picked += before[3:4, tile]
            if last:
                log_total = jnp.log(total)
                out[0:1, tile] = picked - (highest + log_total)
                out[1:2, tile] = log_total - weighted / total
            else:
                out[0:1, tile] = highest
                out[1:2, tile] = total
                out[2:3, tile] = weighted
                out[3:4, tile] = picked
        return carry

    lax.fori_loop(0, hidden.shape[0] // (TILE * UNROLL), body, 0)


def chunk_stats(place, hidden, part, chosen, pieces, before, base, last):
    frames = hidden.shape[0]
    rows, width = pieces[0].shape
    pairs = len(pieces) // 2
    first = before is None
    args = [place, hidden, part, chosen, *pieces] + ([] if first else [before])
    return pl.pallas_call(
        functools.partial(stats_kernel, pairs, first, last, base),
        in_specs=[SMEM] + [VMEM] * (len(args) - 1),
        out_specs=VMEM,
        out_shape=jax.ShapeDtypeStruct((2 if last else 4, frames), jnp.float32),
        scratch_shapes=[pltpu.VMEM((pairs, width, 2 * rows), jnp.bfloat16)],
        compiler_params=pltpu.CompilerParams(vmem_limit_bytes=12 << 20),
        cost_estimate=pl.CostEstimate(
            flops=4 * pairs * frames * rows * width,
            bytes_accessed=1 << 20,
            transcendentals=frames * width,
        ),
        name="stats",
    )(*args)


def place_kernel(offsets, place, *refs):
    pieces, (confidence, entropy) = refs[:-2], refs[-2:]
    for offset, piece in zip(offsets, pieces):
        row = pl.ds(place[2] ^ offset, 1)
        confidence[row, :] = piece[0:1, :]
        entropy[row, :] = piece[1:2, :]


def put_in_place(place, pieces):
    offsets = sorted(pieces)
    shape = (len(offsets), pieces[0].shape[1])
    return pl.pallas_call(
        functools.partial(place_kernel, offsets),
        in_specs=[SMEM] + [VMEM] * len(offsets),
        out_specs=[VMEM, VMEM],
        out_shape=[jax.ShapeDtypeStruct(shape, jnp.float32)] * 2,
        compiler_params=pltpu.CompilerParams(vmem_limit_bytes=4 << 20),
        name="place",
    )(place, *(pieces[offset] for offset in offsets))


def combine(earlier, later):
    highest = jnp.maximum(earlier[0], later[0])
    early, late = earlier[0] - highest, later[0] - highest
    early_factor, late_factor = jnp.exp(early), jnp.exp(late)
    return (
        highest,
        early_factor * earlier[1] + late_factor * later[1],
        early_factor * (earlier[2] + early * earlier[1])
        + late_factor * (later[2] + late * later[1]),
        earlier[3] + later[3],
    )


def shared_levels(stats, sharers, levels):
    shard = lax.axis_index("codes")
    current = tuple(stats)
    for bit in reversed(range(sharers.bit_length() - 1)):
        mine = shard >> bit & 1
        halves = tuple(piece.reshape(2, -1) for piece in current)
        keep = tuple(jnp.where(mine == 0, half[0], half[1]) for half in halves)
        send = tuple(jnp.where(mine == 0, half[1], half[0]) for half in halves)
        current = combine(keep, tuple(flip(piece, "codes", bit) for piece in send))
    highest, total, weighted, picked = current
    log_total = jnp.log(total)
    results = (picked - (highest + log_total), log_total - weighted / total)
    return tuple(
        lax.all_gather(result, "codes", axis=0, tiled=True).reshape(levels, -1)
        for result in results
    )


def on_device(hidden, head, chosen):
    columns = head.shape[1]
    levels = chosen.shape[0]
    frame_count, code_count = lax.axis_size("frames"), lax.axis_size("codes")
    sharers = max(CODES // columns, 1)
    splits = SPLITS if sharers == 1 else (columns,)
    me, shard = lax.axis_index("frames"), lax.axis_index("codes")
    first_column = shard * columns
    place = jnp.stack([me & 1, me >> 1, first_column // CODES, first_column % CODES])
    place = place.astype(jnp.int32)
    far_bits = list(reversed(range(1, frame_count.bit_length() - 1)))

    chunks, low = [], 0
    for width in splits:
        chunks.append(head[:, low : low + width])
        low += width
    sibling = flip(head, "frames", 0)
    far = []
    for chunk in chunks:
        pieces = spread({0: chunk}, "frames", far_bits)
        del pieces[0]
        far.append(pieces)
    hidden = pltpu.with_memory_space_constraint(hidden, pltpu.VMEM)
    parts = partial_logits(place, hidden, head, sibling, splits)
    stats, base = None, 0
    for index, pieces in enumerate(far):
        ordered = []
        for offset in sorted(pieces):
            ordered += [pieces[offset], flip(pieces[offset], "frames", 0)]
        last = index == len(far) - 1 and sharers == 1
        stats = chunk_stats(
            place, hidden, parts[index], chosen, ordered, stats, base, last
        )
        base += splits[index]
    if sharers > 1:
        return shared_levels(stats, sharers, levels)
    bits = reversed(range(code_count.bit_length() - 1))
    return tuple(put_in_place(place, spread({0: stats}, "codes", bits)))


def solution(mesh):
    placed = (P("frames", None), P("frames", "codes"), P(None, "frames"))
    return jax.shard_map(
        on_device,
        mesh=mesh,
        in_specs=placed,
        out_specs=(P(None, "frames"), P(None, "frames")),
        check_vma=False,
    )
```
